512 devices in a mesh: tm: 16 (over y_lo, x, core), space: 32 (over y_hi, z).
Axes of the slice: x: 4, y: 8 (y_hi: 4, y_lo: 2; y = y_hi * 2 + y_lo), z: 8, core: 2. Of those that a mesh axis runs over, the one named last changes fastest.
Arguments:
- rhs_nodes: bfloat16 [16, 384, 4096], P('tm', None, 'space'), may hold values from -6 to 6
- rhs_arrow: float32 [384, 512], replicated, may hold values from -6 to 6
- coupling: bfloat16 [16, 4096, 4096], P('tm', 'space'), may hold values from -0.25 to 0.25
- pattern: int32 [16, 32, 32], P('tm', 'space'), may hold values 0 or 1
- pivot_inverse: bfloat16 [16, 4096, 4096], P('tm', 'space'), may hold values from -0.09375 to 0.09375
- arrow_factor: bfloat16 [16, 512, 4096], P('tm', None, 'space'), may hold values from -0.09375 to 0.09375
- tip_inverse: bfloat16 [512, 512], replicated, may hold values from -0.25 to 0.25
Outputs:
- solved: bfloat16 [16, 384, 4096], P('tm', None, 'space')
- arrow_solved: float32 [384, 512], replicated
The draws below stay inside these ranges and needn't reach their ends.
All inputs are finite; a program needn't handle non-finite values. No bound on the sum of `pattern` on one device may be relied on, other than what follows from the above.
Results may differ from the reference program's by a relative error of at most 0.015.
Values may be sent and summed in bfloat16 or wider, within the bound.
No kernel may reach another device: no remote copies, remote signals or barrier semaphores. Data moves between devices by JAX's collectives and lax.ppermute only.
A program may use at most 64 MiB of HBM per device.

```python
import jax
import jax.numpy as jnp
from jax import lax

NODES = 4096
ARROW = 512
TILE = 128
RHS = 384
STEPS = 16


def with_ends(result, stream_key, least, largest):
    place = [jax.random.randint(jax.random.fold_in(stream_key, axis), (), 0, length) for axis, length in enumerate(result.shape)]
    widest = result.shape.index(max(result.shape))
    neighbour = place[:widest] + [(place[widest] + 1) % result.shape[widest]] + place[widest + 1:]
    return result.at[tuple(place)].set(least).at[tuple(neighbour)].set(largest)


def levels(own_key, dims, shards, smallest, largest):
    factor_of, own = 1.0, jax.random.fold_in(own_key, 6)
    for axis_at, blocks in shards:
        heights = jnp.exp(jax.random.uniform(jax.random.fold_in(own, axis_at), (blocks,), jnp.float32, smallest / len(shards), largest / len(shards)))
        factor_of = factor_of * jnp.repeat(heights, dims[axis_at] // blocks).reshape([-1 if axis == axis_at else 1 for axis in range(len(dims))])
    return factor_of


def noise(stream_key, dims, deviation, limit, shards=(), kind=jnp.bfloat16):
    values = deviation * jax.random.normal(stream_key, dims, jnp.float32)
    if shards:
        values = values * levels(stream_key, dims, shards, -0.22, 0.18)
    return jnp.clip(values, -limit, limit).astype(kind)


def setup_inputs(seed: int = 0) -> dict:
    key_list = jax.random.split(jax.random.key(seed), 8)
    rhs_nodes = noise(key_list[0], (STEPS, RHS, NODES), 1.0, 6.0, ((0, 16), (2, 32)))
    rhs_arrow = noise(key_list[1], (RHS, ARROW), 1.0, 6.0, (), jnp.float32)
    coupling = noise(key_list[2], (STEPS, NODES, NODES), (0.9 * (0.75 * NODES) ** -0.5), 0.25, ((0, 16), (1, 32)))
    pattern = with_ends((jax.random.randint(key_list[3], (STEPS, NODES // TILE, NODES // TILE), 0, 4) < 3).astype(jnp.int32), jax.random.fold_in(key_list[3], 1), 0, 1)
    pivot_inverse = noise(key_list[4], (STEPS, NODES, NODES), NODES ** -0.5, 0.09375, ((0, 16), (1, 32)))
    arrow_factor = noise(key_list[5], (STEPS, ARROW, NODES), ((STEPS * NODES / 3) ** -0.5), 0.09375, ((0, 16), (2, 32)))
    tip_inverse = noise(key_list[6], (ARROW, ARROW), ARROW ** -0.5, 0.25)
    return {"rhs_nodes": rhs_nodes, "rhs_arrow": rhs_arrow, "coupling": coupling, "pattern": pattern, "pivot_inverse": pivot_inverse, "arrow_factor": arrow_factor, "tip_inverse": tip_inverse}


def reference(rhs_nodes, rhs_arrow, coupling, pattern, pivot_inverse, arrow_factor, tip_inverse):
    tile_count = NODES // TILE

    def one_step(carry, inputs):
        previous, total = carry
        source, coupled, tiles, pivots, arrows = inputs
        weights = tiles.astype(coupled.dtype)
        masked = (coupled.reshape(tile_count, TILE, tile_count, TILE) * weights[:, None, :, None]).reshape(NODES, NODES)
        linked = jnp.dot(previous, masked.T, preferred_element_type=jnp.float32)
        fresh = (source.astype(jnp.float32) - linked).astype(jnp.bfloat16)
        solved_step = jnp.dot(fresh, pivots.T, preferred_element_type=jnp.float32).astype(jnp.bfloat16)
        total = total + jnp.dot(fresh, arrows.T, preferred_element_type=jnp.float32)
        return (fresh, total), solved_step

    start = (jnp.zeros((RHS, NODES), jnp.bfloat16), jnp.zeros((RHS, ARROW), jnp.float32))
    (last, arrow_sum), solved = lax.scan(one_step, start, (rhs_nodes, coupling, pattern, pivot_inverse, arrow_factor))
    rest = (rhs_arrow - arrow_sum).astype(jnp.bfloat16)
    arrow_solved = jnp.dot(rest, tip_inverse.T, preferred_element_type=jnp.float32)
    return solved, arrow_solved
```

```python
import jax
import jax.numpy as jnp
from jax import lax
from jax.sharding import PartitionSpec as P

TILE = 128
CONTRACT = (((1,), (1,)), ((), ()))


def spread(value, axis):
    count = lax.axis_size(axis)
    copies = jnp.broadcast_to(value[None], (count, *value.shape))
    return lax.all_to_all(copies, axis, 0, 0)


def per_device(rhs_nodes, rhs_arrow, coupling, pattern, pivot_inverse, arrow_factor, tip_inverse):
    _, local_rows, node_count = coupling.shape
    rhs_count = rhs_nodes.shape[1]
    arrow_count = arrow_factor.shape[1]
    steps = lax.axis_size("tm")
    blocks = lax.axis_size("space")
    width = rhs_count // steps
    arrow_rows = arrow_count // blocks
    section = lax.axis_index("tm")
    block = lax.axis_index("space")

    weights = pattern.astype(jnp.bfloat16)[:, :, None, :, None]
    masked = (coupling.reshape(1, local_rows // TILE, TILE, node_count // TILE, TILE) * weights).reshape(
        1, local_rows, node_count
    )
    links = lax.all_gather(masked, "tm", axis=0, tiled=True)
    source = lax.all_to_all(rhs_nodes.reshape(steps, width, local_rows), "tm", 0, 0)
    arrows = lax.all_to_all(arrow_factor.reshape(blocks, arrow_rows, local_rows), "space", 0, 0)
    arrows = arrows.transpose(1, 0, 2).reshape(1, arrow_rows, node_count)
    outputs = lax.all_gather(jnp.concatenate([pivot_inverse, arrows], 1), "tm", axis=0, tiled=True)

    previous = jnp.zeros((width, node_count), jnp.bfloat16)
    history = []
    for step in range(steps):
        linked = lax.dot_general(previous, links[step], CONTRACT, preferred_element_type=jnp.float32)
        fresh = (source[step].astype(jnp.float32) - linked).astype(jnp.bfloat16)
        previous = spread(fresh, "space").transpose(1, 0, 2).reshape(width, node_count)
        history.append(previous)
    whole = jnp.stack(history)
    results = jnp.einsum("trm,tqm->trq", whole, outputs, preferred_element_type=jnp.float32)
    solved = results[:, :, :local_rows].astype(jnp.bfloat16)
    arrow_sum = jnp.sum(results[:, :, local_rows:], 0)

    own = lax.dynamic_slice(rhs_arrow, (section * width, block * arrow_rows), (width, arrow_rows))
    rest = spread((own - arrow_sum).astype(jnp.bfloat16), "space")
    rest = rest.transpose(1, 0, 2).reshape(width, arrow_count)
    rest = spread(rest, "tm").reshape(rhs_count, arrow_count)
    arrow_solved = lax.dot_general(rest, tip_inverse, CONTRACT, preferred_element_type=jnp.float32)
    solved = lax.all_to_all(solved, "tm", 0, 0).reshape(1, rhs_count, local_rows)
    return (solved, arrow_solved)


def solution(mesh):
    placed = (
        P("tm", None, "space"),
        P(),
        P("tm", "space", None),
        P("tm", "space", None),
        P("tm", "space", None),
        P("tm", None, "space"),
        P(),
    )
    return jax.shard_map(
        per_device,
        mesh=mesh,
        in_specs=placed,
        out_specs=(P("tm", None, "space"), P()),
        check_vma=False,
    )
```

```python
import jax
import jax.numpy as jnp
import numpy as np
from jax import lax
from jax.sharding import Mesh
from jax.sharding import PartitionSpec as P

TILE = 128
CONTRACT = (((1,), (1,)), ((), ()))
AXES = ("yl", "x", "c", "yh", "z")
SIZES = (2, 4, 2, 4, 8)
DEAL = ("yl", "x")
COPY = ("c", "z")
CHAIN = ("yl", "x", "yh")
EARLY = 2


def spread(value, axis):
    count = lax.axis_size(axis)
    copies = jnp.broadcast_to(value[None], (count, *value.shape))
    return lax.all_to_all(copies, axis, 0, 0)


def reorder(rows, deal, piece):
    source = np.arange(TILE)
    upper, lower, blocks = 4, 8, deal
    one = jnp.arange(TILE) // piece
    low = jnp.arange(TILE) % piece
    hot = (
        (one[None, :, None, None] == jnp.arange(blocks)[None, None, :, None])
        & (jnp.arange(lower)[:, None, None, None] == one[None, None, None, :])
        & (low[None, :, None, None] == low[None, None, None, :])
    ).astype(jnp.bfloat16)
    del source
    moved = jnp.einsum(
        "ryzl,zlum->ruym",
        rows.reshape(rows.shape[0], upper, lower, TILE),
        hot,
        preferred_element_type=jnp.float32,
    )
    return moved.astype(jnp.bfloat16).reshape(rows.shape)


def per_device(rhs_nodes, rhs_arrow, coupling, pattern, pivot_inverse, arrow_factor, tip_inverse):
    _, local_rows, node_count = coupling.shape
    rhs_count = rhs_nodes.shape[1]
    arrow_count = arrow_factor.shape[1]
    deal, copies, group = (lax.axis_size(axes) for axes in (DEAL, COPY, CHAIN))
    cores, lower = lax.axis_size("c"), lax.axis_size("z")
    steps = deal * cores
    piece = local_rows // deal
    width = rhs_count // copies
    arrow_rows = arrow_count // group
    mine = lax.axis_index(COPY)

    weights = pattern.astype(jnp.bfloat16)[0, :, None, :, None]
    masked = (coupling.reshape(local_rows // TILE, TILE, node_count // TILE, TILE) * weights).reshape(
        local_rows, node_count
    )
    rows = jnp.concatenate([reorder(masked, deal, piece), rhs_nodes[0].T], 1)
    rows = lax.all_to_all(rows.reshape(deal, piece, -1), DEAL, 0, 0)
    early = spread(rows[:EARLY], COPY)
    late = lax.all_gather(rows[EARLY:], COPY, axis=0)
    out_rows = jnp.concatenate([reorder(pivot_inverse[0], deal, piece), arrow_factor[0].T], 1)
    out_rows = lax.all_to_all(out_rows.reshape(deal, piece, -1), DEAL, 0, 0)
    out_rows = lax.all_gather(out_rows, COPY, axis=0)

    def of_step(held, pair, core):
        return held.reshape(cores, lower, *held.shape[1:])[core, :, pair].reshape(local_rows, -1)

    def link_rows(step):
        pair, core = step // cores, step % cores
        return of_step(early, pair, core) if pair < EARLY else of_step(late, pair - EARLY, core)

    select = (jnp.arange(rhs_count)[None] == mine * width + jnp.arange(width)[:, None]).astype(jnp.bfloat16)
    previous = jnp.zeros((width, node_count), jnp.bfloat16)
    history, parts = [], []
    for step in range(steps):
        held = link_rows(step)
        source = lax.dot_general(select, held[:, node_count:], CONTRACT, preferred_element_type=jnp.float32)
        linked = lax.dot_general(previous, held[:, :node_count], CONTRACT, preferred_element_type=jnp.float32)
        fresh = (source - linked).astype(jnp.bfloat16)
        parts.append(fresh)
        previous = spread(fresh, CHAIN).transpose(1, 0, 2).reshape(width, node_count)
        history.append(previous)

    terms = jnp.zeros((arrow_count, width), jnp.float32)
    solved = []
    for step in range(steps):
        held = of_step(out_rows, step // cores, step % cores)
        terms = terms + lax.dot_general(
            held[:, node_count:], parts[step], (((0,), (1,)), ((), ())), preferred_element_type=jnp.float32
        )
        result = lax.dot_general(
            held[:, :node_count], history[step], CONTRACT, preferred_element_type=jnp.float32
        )
        solved.append(result.astype(jnp.bfloat16))

    place = lax.axis_index(CHAIN)
    own = lax.dynamic_slice(rhs_arrow, (mine * width, place * arrow_rows), (width, arrow_rows)).T
    terms = lax.all_to_all(terms.reshape(group, arrow_rows, width), CHAIN, 0, 0)
    rest = (own - jnp.sum(terms, 0)).astype(jnp.bfloat16)
    rest = spread(rest, CHAIN).reshape(arrow_count, width)
    rest = spread(rest, COPY)
    arrow_solved = jnp.einsum("gar,ba->grb", rest, tip_inverse, preferred_element_type=jnp.float32)
    arrow_solved = arrow_solved.reshape(rhs_count, arrow_count)

    solved = jnp.stack(solved).reshape(deal, cores, lower, piece, width)
    solved = solved.transpose(1, 2, 0, 3, 4).reshape(copies, deal, piece, width)
    solved = lax.all_to_all(solved, COPY, 0, 0).transpose(1, 0, 2, 3)
    solved = lax.all_to_all(solved, DEAL, 0, 0)
    solved = solved.transpose(1, 3, 0, 2).reshape(1, rhs_count, local_rows)
    return (solved, arrow_solved)


def solution(mesh):
    fine = Mesh(mesh.devices.reshape(SIZES), AXES)
    steps, nodes = ("yl", "x", "c"), ("yh", "z")
    placed = (
        P(steps, None, nodes),
        P(),
        P(steps, nodes, None),
        P(steps, nodes, None),
        P(steps, nodes, None),
        P(steps, None, nodes),
        P(),
    )
    return jax.shard_map(
        per_device,
        mesh=fine,
        in_specs=placed,
        out_specs=(P(steps, None, nodes), P()),
        check_vma=False,
    )
```

```python
import jax
import jax.numpy as jnp
from jax import lax
from jax.sharding import PartitionSpec as P

TILE = 128
CONTRACT = (((1,), (1,)), ((), ()))


def product(left, right):
    return lax.dot_general(left, right, CONTRACT, preferred_element_type=jnp.float32)


def spread(value, axis):
    count = lax.axis_size(axis)
    copies = jnp.broadcast_to(value[None], (count, *value.shape))
    return lax.all_to_all(copies, axis, 0, 0)


def per_device(rhs_nodes, rhs_arrow, coupling, pattern, pivot_inverse, arrow_factor, tip_inverse):
    _, local_rows, node_count = coupling.shape
    rhs_count = rhs_nodes.shape[1]
    arrow_count = arrow_factor.shape[1]
    steps = lax.axis_size("tm")
    blocks = lax.axis_size("space")
    width = rhs_count // steps
    arrow_rows = arrow_count // blocks
    section = lax.axis_index("tm")
    block = lax.axis_index("space")

    weights = pattern.astype(jnp.bfloat16)[:, :, None, :, None]
    masked = (coupling.reshape(1, local_rows // TILE, TILE, node_count // TILE, TILE) * weights).reshape(
        1, local_rows, node_count
    )
    links = lax.all_gather(masked, "tm", axis=0, tiled=True)
    source = lax.all_to_all(rhs_nodes.reshape(steps, width, local_rows), "tm", 0, 0)
    arrows = lax.all_to_all(arrow_factor.reshape(blocks, arrow_rows, local_rows), "space", 0, 0)
    arrows = arrows.transpose(1, 0, 2).reshape(1, arrow_rows, node_count)
    outputs = lax.all_gather(jnp.concatenate([pivot_inverse, arrows], 1), "tm", axis=0, tiled=True)

    previous = jnp.zeros((width, node_count), jnp.bfloat16)
    history = []
    for step in range(steps):
        linked = product(previous, links[step])
        fresh = (source[step].astype(jnp.float32) - linked).astype(jnp.bfloat16)
        previous = spread(fresh, "space").transpose(1, 0, 2).reshape(width, node_count)
        history.append(previous)
    solved = [product(history[step], outputs[step, :local_rows]).astype(jnp.bfloat16) for step in range(steps)]
    terms = [product(outputs[step, local_rows:], history[step]) for step in range(steps)]

    own = lax.dynamic_slice(rhs_arrow, (section * width, block * arrow_rows), (width, arrow_rows)).T
    rest = spread((own - sum(terms)).astype(jnp.bfloat16), "space").reshape(arrow_count, width).T
    parts = arrow_count // TILE
    rest = rest.reshape(width, parts, TILE).transpose(1, 0, 2).reshape(parts * width, TILE)
    sent = jnp.stack([jnp.concatenate([value, rest], 0) for value in solved])
    arrived = lax.all_to_all(sent, "tm", 0, 0)
    rest = arrived[:, width:].reshape(steps, parts, width, TILE)
    arrow_solved = sum(
        product(rest[:, part].reshape(rhs_count, TILE), tip_inverse[:, part * TILE : (part + 1) * TILE])
        for part in range(parts)
    )
    return (arrived[:, :width].reshape(1, rhs_count, local_rows), arrow_solved)


def solution(mesh):
    placed = (
        P("tm", None, "space"),
        P(),
        P("tm", "space", None),
        P("tm", "space", None),
        P("tm", "space", None),
        P("tm", None, "space"),
        P(),
    )
    return jax.shard_map(
        per_device,
        mesh=mesh,
        in_specs=placed,
        out_specs=(P("tm", None, "space"), P()),
        check_vma=False,
    )
```

```python
import jax
import jax.numpy as jnp
from jax import lax
from jax.sharding import PartitionSpec as P

TILE = 128
CONTRACT = (((1,), (1,)), ((), ()))


def product(left, right):
    return lax.dot_general(left, right, CONTRACT, preferred_element_type=jnp.float32)


def spread(value, axis):
    count = lax.axis_size(axis)
    copies = jnp.broadcast_to(value[None], (count, *value.shape))
    return lax.all_to_all(copies, axis, 0, 0)


def per_device(rhs_nodes, rhs_arrow, coupling, pattern, pivot_inverse, arrow_factor, tip_inverse):
    _, local_rows, node_count = coupling.shape
    rhs_count = rhs_nodes.shape[1]
    arrow_count = arrow_factor.shape[1]
    steps = lax.axis_size("tm")
    blocks = lax.axis_size("space")
    width = rhs_count // steps
    arrow_rows = arrow_count // blocks
    section = lax.axis_index("tm")
    block = lax.axis_index("space")

    weights = pattern.astype(jnp.bfloat16)[:, :, None, :, None]
    masked = (coupling.reshape(1, local_rows // TILE, TILE, node_count // TILE, TILE) * weights).reshape(
        1, local_rows, node_count
    )
    links = lax.all_gather(masked, "tm", axis=0, tiled=True)
    initial = jnp.zeros((rhs_count, node_count), jnp.bfloat16)
    entering = jnp.where(section == 0, product(initial, masked[0]), 0.0)
    forcing = rhs_nodes[0].astype(jnp.float32) - entering
    source = lax.all_to_all(forcing.astype(jnp.bfloat16).reshape(steps, width, local_rows), "tm", 0, 0)
    arrows = lax.all_to_all(arrow_factor.reshape(blocks, arrow_rows, local_rows), "space", 0, 0)
    arrows = arrows.transpose(1, 0, 2).reshape(1, arrow_rows, node_count)
    outputs = lax.all_gather(jnp.concatenate([pivot_inverse, arrows], 1), "tm", axis=0, tiled=True)

    history = []
    fresh = source[0]
    for step in range(steps):
        if step > 0:
            linked = product(previous, lax.optimization_barrier(links[step]))
            fresh = (source[step].astype(jnp.float32) - linked).astype(jnp.bfloat16)
        previous = spread(fresh, "space").transpose(1, 0, 2).reshape(width, node_count)
        history.append(previous)
    solved, terms = [], []
    for step in range(steps):
        held = lax.optimization_barrier(outputs[step])
        solved.append(product(history[step], held[:local_rows]).astype(jnp.bfloat16))
        terms.append(product(held[local_rows:], history[step]))

    own = lax.dynamic_slice(rhs_arrow, (section * width, block * arrow_rows), (width, arrow_rows)).T
    rest = spread((own - sum(terms)).astype(jnp.bfloat16), "space").reshape(arrow_count, width).T
    parts = arrow_count // TILE
    rest = rest.reshape(width, parts, TILE).transpose(1, 0, 2).reshape(parts * width, TILE)
    sent = jnp.stack([jnp.concatenate([value, rest], 0) for value in solved])
    arrived = lax.all_to_all(sent, "tm", 0, 0)
    rest = arrived[:, width:].reshape(steps, parts, width, TILE)
    arrow_solved = sum(
        product(rest[:, part].reshape(rhs_count, TILE), tip_inverse[:, part * TILE : (part + 1) * TILE])
        for part in range(parts)
    )
    return (arrived[:, :width].reshape(1, rhs_count, local_rows), arrow_solved)


def solution(mesh):
    placed = (
        P("tm", None, "space"),
        P(),
        P("tm", "space", None),
        P("tm", "space", None),
        P("tm", "space", None),
        P("tm", None, "space"),
        P(),
    )
    return jax.shard_map(
        per_device,
        mesh=mesh,
        in_specs=placed,
        out_specs=(P("tm", None, "space"), P()),
        check_vma=False,
    )
```

```python
import jax
import jax.numpy as jnp
import numpy as np
from jax import lax
from jax.sharding import Mesh
from jax.sharding import PartitionSpec as P

TILE = 128
CONTRACT = (((1,), (1,)), ((), ()))
AXES = ("yl", "x", "c", "yh", "z")
SIZES = (2, 4, 2, 4, 8)
DEAL = ("yl", "x")
COPY = ("c", "z")
CHAIN = ("yl", "x", "yh")
CHUNKS = (2, 3, 3)
OUT_AFTER = 5


def spread(value, axis):
    count = lax.axis_size(axis)
    copies = jnp.broadcast_to(value[None], (count, *value.shape))
    return lax.all_to_all(copies, axis, 0, 0)


def chain_order(deal, lower, piece):
    old = jnp.arange(lower * deal * piece).reshape(lower, deal, piece)
    new = old.transpose(1, 0, 2).reshape(deal, lower * piece)
    return (old.reshape(lower, deal * piece, 1, 1) == new).astype(jnp.bfloat16)


def product(left, right):
    return lax.dot_general(left, right, CONTRACT, preferred_element_type=jnp.float32)


def per_device(rhs_nodes, rhs_arrow, coupling, pattern, pivot_inverse, arrow_factor, tip_inverse):
    _, local_rows, node_count = coupling.shape
    rhs_count = rhs_nodes.shape[1]
    arrow_count = arrow_factor.shape[1]
    deal, copies, group = (lax.axis_size(axes) for axes in (DEAL, COPY, CHAIN))
    cores, lower = lax.axis_size("c"), lax.axis_size("z")
    steps = deal * cores
    piece = local_rows // deal
    width = rhs_count // copies
    arrow_rows = arrow_count // group
    mine = lax.axis_index(COPY)

    weights = pattern.astype(jnp.bfloat16)[0, :, None, :, None]
    masked = (coupling.reshape(local_rows // TILE, TILE, node_count // TILE, TILE) * weights).reshape(
        local_rows, node_count
    )
    upper = lax.axis_size("yh")
    order = chain_order(deal, lower, piece)

    def reorder(rows):
        moved = jnp.einsum(
            "ryzl,zlum->ruym",
            rows.reshape(local_rows, upper, lower, TILE),
            order,
            preferred_element_type=jnp.float32,
        )
        return moved.astype(jnp.bfloat16).reshape(local_rows, node_count)

    rows = jnp.concatenate([reorder(masked), rhs_nodes[0].T], 1)
    rows = lax.all_to_all(rows.reshape(deal, piece, -1), DEAL, 0, 0)
    first, second, third = jnp.split(rows, np.cumsum(CHUNKS)[:-1])
    links = [lax.all_gather(first, COPY, axis=0)]
    out_rows = lax.all_to_all(reorder(pivot_inverse[0]).reshape(deal, piece, -1), DEAL, 0, 0)
    second, out_rows = lax.optimization_barrier((second, out_rows))
    links.append(lax.all_gather(second, COPY, axis=0))
    arrows = lax.all_to_all(arrow_factor.reshape(group, arrow_rows, TILE), CHAIN, 0, 0)
    third, arrows = lax.optimization_barrier((third, arrows))
    links.append(lax.all_gather(third, COPY, axis=0))

    def of_step(held, pair, core):
        return held.reshape(cores, lower, *held.shape[1:])[core, :, pair].reshape(local_rows, -1)

    def link_rows(step):
        pair, core = step // cores, step % cores
        for chunk, pairs in enumerate(CHUNKS):
            if pair < pairs:
                return of_step(links[chunk], pair, core)
            pair -= pairs

    select = (jnp.arange(rhs_count)[None] == mine * width + jnp.arange(width)[:, None]).astype(jnp.bfloat16)
    previous = jnp.zeros((width, node_count), jnp.bfloat16)
    history = []
    for step in range(steps):
        held = link_rows(step)
        source = product(select, held[:, node_count:])
        linked = product(previous, held[:, :node_count])
        fresh = (source - linked).astype(jnp.bfloat16)
        if step == OUT_AFTER:
            fresh, out_rows, arrows = lax.optimization_barrier((fresh, out_rows, arrows))
            out_rows = lax.all_gather(out_rows, COPY, axis=0)
            arrows = lax.all_gather(arrows.reshape(deal, upper, arrow_rows, TILE), COPY, axis=0)
        previous = spread(fresh, CHAIN).transpose(1, 0, 2).reshape(width, node_count)
        history.append(previous)
    arrows = arrows.reshape(cores, lower, deal, upper, arrow_rows, TILE)
    arrows = jnp.einsum("czpyal,zlum->pcauym", arrows, order, preferred_element_type=jnp.float32)
    arrows = arrows.astype(jnp.bfloat16).reshape(steps, arrow_rows, node_count)
    solved = [
        product(history[step], of_step(out_rows, step // cores, step % cores)).astype(jnp.bfloat16)
        for step in range(steps)
    ]
    terms = [product(arrows[step], history[step]) for step in range(steps)]

    place = lax.axis_index(CHAIN)
    own = lax.dynamic_slice(rhs_arrow, (mine * width, place * arrow_rows), (width, arrow_rows)).T
    rest = spread((own - sum(terms)).astype(jnp.bfloat16), CHAIN).reshape(arrow_count, width).T
    parts = arrow_count // TILE
    rest = rest.reshape(width, parts, TILE).transpose(1, 0, 2).reshape(1, parts * width, TILE)

    solved = jnp.stack(solved).reshape(deal, cores, width, lower, piece)
    solved = solved.transpose(1, 3, 2, 0, 4).reshape(copies, width, deal * piece)
    sent = jnp.concatenate([solved, jnp.broadcast_to(rest, (copies, parts * width, TILE))], 1)
    arrived = lax.all_to_all(sent, COPY, 0, 0)
    rest = arrived[:, width:].reshape(copies, parts, width, TILE)
    arrow_solved = sum(
        product(rest[:, part].reshape(rhs_count, TILE), tip_inverse[:, part * TILE : (part + 1) * TILE])
        for part in range(parts)
    )
    solved = arrived[:, :width].reshape(rhs_count, deal, piece).transpose(1, 0, 2)
    solved = lax.all_to_all(solved, DEAL, 0, 0)
    solved = solved.transpose(1, 0, 2).reshape(1, rhs_count, local_rows)
    return (solved, arrow_solved)


def solution(mesh):
    fine = Mesh(mesh.devices.reshape(SIZES), AXES)
    steps, nodes = ("yl", "x", "c"), ("yh", "z")
    placed = (
        P(steps, None, nodes),
        P(),
        P(steps, nodes, None),
        P(steps, nodes, None),
        P(steps, nodes, None),
        P(steps, None, nodes),
        P(),
    )
    return jax.shard_map(
        per_device,
        mesh=fine,
        in_specs=placed,
        out_specs=(P(steps, None, nodes), P()),
        check_vma=False,
    )
```

```python
import jax
import jax.numpy as jnp
import numpy as np
from jax import lax
from jax.sharding import Mesh
from jax.sharding import PartitionSpec as P

TILE = 128
CONTRACT = (((1,), (1,)), ((), ()))
AXES = ("yl", "x", "c", "yh", "z")
SIZES = (2, 4, 2, 4, 8)
DEAL = ("yl", "x")
COPY = ("c", "z")
CHAIN = ("yl", "x", "yh")
CHUNKS = (2, 2, 4)
OUT_AFTER = 2


def spread(value, axis):
    count = lax.axis_size(axis)
    copies = jnp.broadcast_to(value[None], (count, *value.shape))
    return lax.all_to_all(copies, axis, 0, 0)


def chain_order(deal, lower, piece):
    old = jnp.arange(lower * deal * piece).reshape(lower, deal, piece)
    new = old.transpose(1, 0, 2).reshape(deal, lower * piece)
    return (old.reshape(lower, deal * piece, 1, 1) == new).astype(jnp.bfloat16)


def product(left, right):
    return lax.dot_general(left, right, CONTRACT, preferred_element_type=jnp.float32)


def per_device(rhs_nodes, rhs_arrow, coupling, pattern, pivot_inverse, arrow_factor, tip_inverse):
    _, local_rows, node_count = coupling.shape
    rhs_count = rhs_nodes.shape[1]
    arrow_count = arrow_factor.shape[1]
    deal, copies, group = (lax.axis_size(axes) for axes in (DEAL, COPY, CHAIN))
    cores, lower = lax.axis_size("c"), lax.axis_size("z")
    steps = deal * cores
    piece = local_rows // deal
    width = rhs_count // copies
    mine = lax.axis_index(COPY)

    weights = pattern.astype(jnp.bfloat16)[0, :, None, :, None]
    masked = (coupling.reshape(local_rows // TILE, TILE, node_count // TILE, TILE) * weights).reshape(
        local_rows, node_count
    )
    upper = lax.axis_size("yh")
    order = chain_order(deal, lower, piece)

    def reorder(rows):
        moved = jnp.einsum(
            "ryzl,zlum->ruym",
            rows.reshape(local_rows, upper, lower, TILE),
            order,
            preferred_element_type=jnp.float32,
        )
        return moved.astype(jnp.bfloat16).reshape(local_rows, node_count)

    initial = jnp.zeros((8, node_count), jnp.bfloat16)
    entering = jnp.where(lax.axis_index(DEAL + ("c",)) == 0, product(masked, initial)[:, :1], 0.0)
    forcing = (rhs_nodes[0].T.astype(jnp.float32) - entering).astype(jnp.bfloat16)
    rows = jnp.concatenate([reorder(masked), forcing], 1)
    rows = lax.all_to_all(rows.reshape(deal, piece, -1), DEAL, 0, 0)
    forcing = rows[:, :, node_count:].reshape(deal * piece, copies, width).transpose(1, 0, 2)
    first, second, third = jnp.split(rows[:, :, :node_count], np.cumsum(CHUNKS)[:-1])
    links = [lax.all_gather(first, COPY, axis=0)]
    forcing = lax.all_to_all(forcing, COPY, 0, 0).reshape(cores, lower, deal, piece, width)
    forcing = forcing.transpose(2, 0, 4, 1, 3).reshape(steps, width, local_rows)
    previous = spread(forcing[0], CHAIN)
    second, previous = lax.optimization_barrier((second, previous))
    links.append(lax.all_gather(second, COPY, axis=0))
    out_rows = jnp.concatenate([reorder(pivot_inverse[0]), arrow_factor[0].T], 1)
    out_rows = lax.all_to_all(out_rows.reshape(deal, piece, -1), DEAL, 0, 0)
    third, out_rows = lax.optimization_barrier((third, out_rows))
    links.append(lax.all_gather(third, COPY, axis=0))

    def of_step(held, pair, core):
        return held.reshape(cores, lower, *held.shape[1:])[core, :, pair].reshape(local_rows, -1)

    def link_rows(step):
        pair, core = step // cores, step % cores
        for chunk, pairs in enumerate(CHUNKS):
            if pair < pairs:
                return of_step(links[chunk], pair, core)
            pair -= pairs

    def whole(gathered):
        return gathered.transpose(1, 0, 2).reshape(width, node_count)

    parts = [forcing[0]]
    history = [whole(previous)]
    for step in range(1, steps):
        linked = product(history[-1], link_rows(step))
        fresh = (forcing[step].astype(jnp.float32) - linked).astype(jnp.bfloat16)
        if step == OUT_AFTER:
            fresh, out_rows = lax.optimization_barrier((fresh, out_rows))
            out_rows = lax.all_gather(out_rows, COPY, axis=0)
        parts.append(fresh)
        if step < steps - 1:
            history.append(whole(spread(fresh, CHAIN)))

    held = [of_step(out_rows, step // cores, step % cores) for step in range(steps)]
    terms = jnp.zeros((width, arrow_count), jnp.float32)
    for step in range(steps):
        terms = terms + jnp.dot(parts[step], held[step][:, node_count:], preferred_element_type=jnp.float32)
    tiles = arrow_count // TILE
    share = width // (group // tiles)
    terms = terms.reshape(group // tiles, share, tiles, TILE).transpose(0, 2, 1, 3).reshape(group, share, TILE)
    last = jnp.broadcast_to(parts[-1].astype(jnp.float32), (group, width, local_rows))
    arrived = lax.all_to_all(jnp.concatenate([last, terms], 1), CHAIN, 0, 0)
    history.append(whole(arrived[:, :width].astype(jnp.bfloat16)))
    place = lax.axis_index(CHAIN)
    corner = (mine * width + place // tiles * share, place % tiles * TILE)
    own = lax.dynamic_slice(rhs_arrow, corner, (share, TILE))
    rest = spread((own - jnp.sum(arrived[:, width:], 0)).astype(jnp.bfloat16), CHAIN)
    rest = rest.reshape(group // tiles, tiles, share, TILE).transpose(1, 0, 2, 3).reshape(1, tiles * width, TILE)
    solved = [product(history[step], held[step][:, :node_count]).astype(jnp.bfloat16) for step in range(steps)]

    solved = jnp.stack(solved).reshape(deal, cores, width, lower, piece)
    solved = solved.transpose(1, 3, 2, 0, 4).reshape(copies, width, deal * piece)
    sent = jnp.concatenate([solved, jnp.broadcast_to(rest, (copies, tiles * width, TILE))], 1)
    arrived = lax.all_to_all(sent, COPY, 0, 0)
    rest = arrived[:, width:].reshape(copies, tiles, width, TILE)
    arrow_solved = sum(
        product(rest[:, part].reshape(rhs_count, TILE), tip_inverse[:, part * TILE : (part + 1) * TILE])
        for part in range(tiles)
    )
    solved = arrived[:, :width].reshape(rhs_count, deal, piece).transpose(1, 0, 2)
    solved = lax.all_to_all(solved, DEAL, 0, 0)
    solved = solved.transpose(1, 0, 2).reshape(1, rhs_count, local_rows)
    return (solved, arrow_solved)


def solution(mesh):
    fine = Mesh(mesh.devices.reshape(SIZES), AXES)
    steps, nodes = ("yl", "x", "c"), ("yh", "z")
    placed = (
        P(steps, None, nodes),
        P(),
        P(steps, nodes, None),
        P(steps, nodes, None),
        P(steps, nodes, None),
        P(steps, None, nodes),
        P(),
    )
    return jax.shard_map(
        per_device,
        mesh=fine,
        in_specs=placed,
        out_specs=(P(steps, None, nodes), P()),
        check_vma=False,
    )
```

```python
import jax
import jax.numpy as jnp
import numpy as np
from jax import lax
from jax.experimental.layout import Layout, with_layout_constraint
from jax.sharding import Mesh
from jax.sharding import PartitionSpec as P

TILE = 128
CONTRACT = (((1,), (1,)), ((), ()))
AXES = ("yl", "x", "c", "yh", "z")
SIZES = (2, 4, 2, 4, 8)
DEAL = ("yl", "x")
COPY = ("c", "z")
CHAIN = ("yl", "x", "yh")
CHUNKS = (2, 2, 4)
OUT_AFTER = 2


def spread(value, axis):
    count = lax.axis_size(axis)
    copies = jnp.broadcast_to(value[None], (count, *value.shape))
    return lax.all_to_all(copies, axis, 0, 0)


def chain_order(deal, lower, piece):
    old = jnp.arange(lower * deal * piece).reshape(lower, deal, piece)
    new = old.transpose(1, 0, 2).reshape(deal, lower * piece)
    return (old.reshape(lower, deal * piece, 1, 1) == new).astype(jnp.bfloat16)


def product(left, right):
    return lax.dot_general(left, right, CONTRACT, preferred_element_type=jnp.float32)


def per_device(rhs_nodes, rhs_arrow, coupling, pattern, pivot_inverse, arrow_factor, tip_inverse):
    _, local_rows, node_count = coupling.shape
    rhs_count = rhs_nodes.shape[1]
    arrow_count = arrow_factor.shape[1]
    deal, copies, group = (lax.axis_size(axes) for axes in (DEAL, COPY, CHAIN))
    cores, lower = lax.axis_size("c"), lax.axis_size("z")
    steps = deal * cores
    piece = local_rows // deal
    width = rhs_count // copies
    mine = lax.axis_index(COPY)

    weights = pattern.astype(jnp.bfloat16)[0, :, None, :, None]
    masked = (coupling.reshape(local_rows // TILE, TILE, node_count // TILE, TILE) * weights).reshape(
        local_rows, node_count
    )
    upper = lax.axis_size("yh")
    order = chain_order(deal, lower, piece)

    def reorder(rows):
        moved = jnp.einsum(
            "ryzl,zlum->ruym",
            rows.reshape(local_rows, upper, lower, TILE),
            order,
            preferred_element_type=jnp.float32,
        )
        return moved.astype(jnp.bfloat16).reshape(local_rows, node_count)

    initial = jnp.zeros((8, node_count), jnp.bfloat16)
    entering = jnp.where(lax.axis_index(DEAL + ("c",)) == 0, product(masked, initial)[:, :1], 0.0)
    forcing = (rhs_nodes[0].T.astype(jnp.float32) - entering).astype(jnp.bfloat16)
    rows = jnp.concatenate([reorder(masked), forcing, arrow_factor[0].T], 1)
    rows = lax.all_to_all(rows.reshape(deal, piece, -1), DEAL, 0, 0)
    forcing = rows[:, :, node_count : node_count + rhs_count].reshape(deal * piece, copies, width).transpose(1, 0, 2)
    arrows = rows[:, :, node_count + rhs_count :].transpose(1, 0, 2).reshape(1, piece, deal * arrow_count)
    first, second, third = jnp.split(rows[:, :, :node_count], np.cumsum(CHUNKS)[:-1])
    links = [lax.all_gather(first, COPY, axis=0)]
    forcing = lax.all_to_all(forcing, COPY, 0, 0).reshape(cores, lower, deal, piece, width)
    forcing = forcing.transpose(2, 0, 4, 1, 3).reshape(steps, width, local_rows)
    previous = spread(forcing[0], CHAIN)
    second, previous = lax.optimization_barrier((second, previous))
    links.append(lax.all_gather(second, COPY, axis=0))
    third = jnp.concatenate([third, arrows], 0)
    out_rows = with_layout_constraint(reorder(pivot_inverse[0]), Layout((0, 1)))

    def of_step(held, pair, core):
        return held.reshape(cores, lower, *held.shape[1:])[core, :, pair].reshape(local_rows, -1)

    def link_rows(step):
        pair, core = step // cores, step % cores
        for chunk, pairs in enumerate(CHUNKS):
            if pair < pairs:
                return of_step(links[chunk], pair, core)
            pair -= pairs

    def whole(gathered):
        return gathered.transpose(1, 0, 2).reshape(width, node_count)

    parts = [forcing[0]]
    history = [previous]
    for step in range(1, steps):
        linked = product(whole(history[-1]), link_rows(step))
        fresh = (forcing[step].astype(jnp.float32) - linked).astype(jnp.bfloat16)
        if step == 1:
            fresh, third, out_rows = lax.optimization_barrier((fresh, third, out_rows))
            links.append(lax.all_gather(third, COPY, axis=0))
        if step == OUT_AFTER:
            fresh, out_rows = lax.optimization_barrier((fresh, out_rows))
            out_rows = lax.all_gather(out_rows, COPY, axis=0)
        if step == steps - 3:
            fresh, *parts = lax.optimization_barrier((fresh, *parts))
        if step == steps - 2:
            fresh, *history = lax.optimization_barrier((fresh, *history))
        if step == steps - 1:
            fresh, out_rows = lax.optimization_barrier((fresh, out_rows))
        parts.append(fresh)
        if step < steps - 1:
            history.append(spread(fresh, CHAIN))

    terms = jnp.zeros((width, arrow_count), jnp.float32)
    for step in range(steps):
        pair, core = step // cores, step % cores
        columns = slice(pair * arrow_count, (pair + 1) * arrow_count)
        held = of_step(links[-1], CHUNKS[-1], core)[:, columns]
        terms = terms + jnp.dot(parts[step], held, preferred_element_type=jnp.float32)
    tiles = arrow_count // TILE
    share = width // (group // tiles)
    terms = terms.reshape(group // tiles, share, tiles, TILE).transpose(0, 2, 1, 3).reshape(group, share, TILE)
    last = jnp.broadcast_to(parts[-1].astype(jnp.float32), (group, width, local_rows))
    arrived = lax.all_to_all(jnp.concatenate([last, terms], 1), CHAIN, 0, 0)
    history.append(arrived[:, :width].astype(jnp.bfloat16))
    place = lax.axis_index(CHAIN)
    corner = (mine * width + place // tiles * share, place % tiles * TILE)
    own = lax.dynamic_slice(rhs_arrow, corner, (share, TILE))
    rest = (own - jnp.sum(arrived[:, width:], 0)).astype(jnp.bfloat16)
    rest, history[-1] = lax.optimization_barrier((rest, history[-1]))
    rest = spread(rest, CHAIN)
    rest = rest.reshape(group // tiles, tiles, share, TILE).transpose(1, 0, 2, 3).reshape(1, tiles * width, TILE)
    pair = lax.axis_index(DEAL)
    solved = []
    for core in range(cores):
        chosen = history[core]
        for other in range(1, deal):
            chosen = jnp.where(pair == other, history[other * cores + core], chosen)
        held = out_rows[core * lower : (core + 1) * lower].reshape(lower * local_rows, node_count)
        result = product(whole(chosen), held).astype(jnp.bfloat16)
        solved.append(result.reshape(width, lower, local_rows).transpose(1, 0, 2))
    solved = jnp.concatenate(solved, 0)
    sent = jnp.concatenate([solved, jnp.broadcast_to(rest, (copies, tiles * width, TILE))], 1)
    arrived = lax.all_to_all(sent, COPY, 0, 0)
    rest = arrived[:, width:].reshape(copies, tiles, width, TILE)
    arrow_solved = sum(
        product(rest[:, part].reshape(rhs_count, TILE), tip_inverse[:, part * TILE : (part + 1) * TILE])
        for part in range(tiles)
    )
    solved = arrived[:, :width].reshape(1, rhs_count, local_rows)
    return (solved, arrow_solved)


def solution(mesh):
    fine = Mesh(mesh.devices.reshape(SIZES), AXES)
    steps, nodes = ("yl", "x", "c"), ("yh", "z")
    placed = (
        P(steps, None, nodes),
        P(),
        P(steps, nodes, None),
        P(steps, nodes, None),
        P(steps, nodes, None),
        P(steps, None, nodes),
        P(),
    )
    return jax.shard_map(
        per_device,
        mesh=fine,
        in_specs=placed,
        out_specs=(P(steps, None, nodes), P()),
        check_vma=False,
    )
```

```python
import jax
import jax.numpy as jnp
import numpy as np
from jax import lax
from jax.experimental.layout import Layout, with_layout_constraint
from jax.sharding import Mesh
from jax.sharding import PartitionSpec as P

TILE = 128
CONTRACT = (((1,), (1,)), ((), ()))
AXES = ("yl", "x", "c", "yh", "z")
SIZES = (2, 4, 2, 4, 8)
DEAL = ("yl", "x")
COPY = ("c", "z")
CHAIN = ("yl", "x", "yh")
CHUNKS = (2, 3, 3)
OUT_AFTER = 2


def spread(value, axis):
    count = lax.axis_size(axis)
    copies = jnp.broadcast_to(value[None], (count, *value.shape))
    return lax.all_to_all(copies, axis, 0, 0)


def chain_order(deal, lower, piece):
    old = jnp.arange(lower * deal * piece).reshape(lower, deal, piece)
    new = old.transpose(1, 0, 2).reshape(deal, lower * piece)
    return (old.reshape(lower, deal * piece, 1, 1) == new).astype(jnp.bfloat16)


def product(left, right):
    return lax.dot_general(left, right, CONTRACT, preferred_element_type=jnp.float32)


def per_device(rhs_nodes, rhs_arrow, coupling, pattern, pivot_inverse, arrow_factor, tip_inverse):
    _, local_rows, node_count = coupling.shape
    rhs_count = rhs_nodes.shape[1]
    arrow_count = arrow_factor.shape[1]
    deal, copies, group = (lax.axis_size(axes) for axes in (DEAL, COPY, CHAIN))
    cores, lower = lax.axis_size("c"), lax.axis_size("z")
    steps = deal * cores
    piece = local_rows // deal
    width = rhs_count // copies
    mine = lax.axis_index(COPY)

    weights = jnp.repeat(pattern.astype(jnp.bfloat16)[0], TILE, axis=1)
    masked = coupling[0] * weights
    upper = lax.axis_size("yh")
    order = chain_order(deal, lower, piece)

    def reorder(rows):
        span = node_count // upper
        table = order.reshape(span, span)
        moved = [
            jnp.dot(rows[:, at : at + span], table, preferred_element_type=jnp.float32).astype(jnp.bfloat16)
            for at in range(0, node_count, span)
        ]
        return jnp.concatenate([block[:, at : at + TILE] for at in range(0, span, TILE) for block in moved], 1)

    initial = jnp.zeros((8, node_count), jnp.bfloat16)
    entering = jnp.where(lax.axis_index(DEAL + ("c",)) == 0, product(masked, initial)[:, :1], 0.0)
    forcing = (rhs_nodes[0].T.astype(jnp.float32) - entering).astype(jnp.bfloat16)
    rows = jnp.concatenate([reorder(masked), forcing, arrow_factor[0].T], 1)
    rows = lax.all_to_all(rows.reshape(deal, piece, -1), DEAL, 0, 0)
    forcing = rows[:, :, node_count : node_count + rhs_count].reshape(deal * piece, copies, width).transpose(1, 0, 2)
    arrows = rows[:, :, node_count + rhs_count :].transpose(1, 0, 2).reshape(1, piece, deal * arrow_count)
    first, second, third = jnp.split(rows[:, :, :node_count], np.cumsum(CHUNKS)[:-1])
    links = [lax.all_gather(first, COPY, axis=0)]
    forcing = lax.all_to_all(forcing, COPY, 0, 0).reshape(cores, lower, deal, piece, width)
    forcing = forcing.transpose(2, 0, 4, 1, 3).reshape(steps, width, local_rows)
    previous = spread(forcing[0], CHAIN)
    second, previous = lax.optimization_barrier((second, previous))
    links.append(lax.all_gather(second, COPY, axis=0))
    third = jnp.concatenate([third, arrows], 0)
    out_rows = with_layout_constraint(reorder(pivot_inverse[0]), Layout((0, 1)))

    def of_step(held, pair, core):
        return held.reshape(cores, lower, *held.shape[1:])[core, :, pair].reshape(local_rows, -1)

    def link_rows(step):
        pair, core = step // cores, step % cores
        for chunk, pairs in enumerate(CHUNKS):
            if pair < pairs:
                return of_step(links[chunk], pair, core)
            pair -= pairs

    def whole(gathered):
        return gathered.transpose(1, 0, 2).reshape(width, node_count)

    parts = [forcing[0]]
    history = [previous]
    for step in range(1, steps):
        linked = product(whole(history[-1]), link_rows(step))
        fresh = (forcing[step].astype(jnp.float32) - linked).astype(jnp.bfloat16)
        if step == 1:
            fresh, third, out_rows = lax.optimization_barrier((fresh, third, out_rows))
            links.append(lax.all_gather(third, COPY, axis=0))
        if step == OUT_AFTER:
            fresh, out_rows = lax.optimization_barrier((fresh, out_rows))
            out_rows = lax.all_gather(out_rows, COPY, axis=0)
        if step == steps - 3:
            fresh, *parts = lax.optimization_barrier((fresh, *parts))
        if step == steps - 2:
            fresh, *history = lax.optimization_barrier((fresh, *history))
        if step == steps - 1:
            fresh, out_rows = lax.optimization_barrier((fresh, out_rows))
        parts.append(fresh)
        if step < steps - 1:
            history.append(spread(fresh, CHAIN))

    terms = jnp.zeros((width, arrow_count), jnp.float32)
    for step in range(steps):
        pair, core = step // cores, step % cores
        columns = slice(pair * arrow_count, (pair + 1) * arrow_count)
        held = of_step(links[-1], CHUNKS[-1], core)[:, columns]
        terms = terms + jnp.dot(parts[step], held, preferred_element_type=jnp.float32)
    tiles = arrow_count // TILE
    share = width // (group // tiles)
    terms = terms.reshape(group // tiles, share, tiles, TILE).transpose(0, 2, 1, 3).reshape(group, share, TILE)
    last = jnp.broadcast_to(parts[-1].astype(jnp.float32), (group, width, local_rows))
    arrived = lax.all_to_all(jnp.concatenate([last, terms], 1), CHAIN, 0, 0)
    history.append(arrived[:, :width].astype(jnp.bfloat16))
    place = lax.axis_index(CHAIN)
    corner = (mine * width + place // tiles * share, place % tiles * TILE)
    own = lax.dynamic_slice(rhs_arrow, corner, (share, TILE))
    rest = (own - jnp.sum(arrived[:, width:], 0)).astype(jnp.bfloat16)
    rest, history[-1] = lax.optimization_barrier((rest, history[-1]))
    rest = spread(rest, CHAIN)
    rest = rest.reshape(group // tiles, tiles, share, TILE).transpose(1, 0, 2, 3).reshape(1, tiles * width, TILE)
    pair = lax.axis_index(DEAL)
    solved = []
    for core in range(cores):
        chosen = history[core]
        for other in range(1, deal):
            chosen = jnp.where(pair == other, history[other * cores + core], chosen)
        held = out_rows[core * lower : (core + 1) * lower].reshape(lower * local_rows, node_count)
        result = product(whole(chosen), held).astype(jnp.bfloat16)
        solved.append(result.reshape(width, lower, local_rows).transpose(1, 0, 2))
    solved = jnp.concatenate(solved, 0)
    sent = jnp.concatenate([solved, jnp.broadcast_to(rest, (copies, tiles * width, TILE))], 1)
    arrived = lax.all_to_all(sent, COPY, 0, 0)
    rest = arrived[:, width:].reshape(copies, tiles, width, TILE)
    arrow_solved = sum(
        product(rest[:, part].reshape(rhs_count, TILE), tip_inverse[:, part * TILE : (part + 1) * TILE])
        for part in range(tiles)
    )
    solved = arrived[:, :width].reshape(1, rhs_count, local_rows)
    return (solved, arrow_solved)


def solution(mesh):
    fine = Mesh(mesh.devices.reshape(SIZES), AXES)
    steps, nodes = ("yl", "x", "c"), ("yh", "z")
    placed = (
        P(steps, None, nodes),
        P(),
        P(steps, nodes, None),
        P(steps, nodes, None),
        P(steps, nodes, None),
        P(steps, None, nodes),
        P(),
    )
    return jax.shard_map(
        per_device,
        mesh=fine,
        in_specs=placed,
        out_specs=(P(steps, None, nodes), P()),
        check_vma=False,
    )
```
